32 devices in a mesh: row: 8 (over y, x, core), col: 4 (over z).
Axes of the slice: x: 2, y: 2, z: 4, core: 2. Of those that a mesh axis runs over, the one named last changes fastest.
Arguments:
- sample_counts: int32 [64], replicated, may hold values from 100 to 2000
- slot_silo: int32 [64], replicated, may hold values from 0 to 63, each once
- gate_weight: bfloat16 [28672, 8192], P('row', 'col'), may hold values from -3 to 3
- up_weight: bfloat16 [28672, 8192], P('row', 'col'), may hold values from -3 to 3
- down_weight: bfloat16 [8192, 28672], P('row', 'col'), may hold values from -3 to 3
- gate_a: bfloat16 [1024, 8192], P(('row', 'col')), may hold values from -6 to 6
- up_a: bfloat16 [1024, 8192], P(('row', 'col')), may hold values from -6 to 6
- down_a: bfloat16 [1024, 28672], P(('row', 'col')), may hold values from -6 to 6
- gate_b: bfloat16 [1024, 28672], P(('row', 'col')), may hold values from -6 to 6
- up_b: bfloat16 [1024, 28672], P(('row', 'col')), may hold values from -6 to 6
- down_b: bfloat16 [1024, 8192], P(('row', 'col')), may hold values from -6 to 6
Outputs:
- merged_gate: bfloat16 [28672, 8192], P('row', 'col')
- merged_up: bfloat16 [28672, 8192], P('row', 'col')
- merged_down: bfloat16 [8192, 28672], P('row', 'col')
The draws below stay inside these ranges and needn't reach their ends.
Inputs may be any that keep to these rules, and one draw needn't show every extreme that they name: `slot_silo`: a permutation of the silos.
All inputs are finite; a program needn't handle non-finite values.
Results may differ from the reference program's by a relative error of at most 0.0043.
Values may be sent and summed in bfloat16 or wider, within the bound.
No kernel may reach another device: no remote copies, remote signals or barrier semaphores. Data moves between devices by JAX's collectives and lax.ppermute only.
A program may use at most 256 MiB of HBM per device.

```python
import jax
import jax.numpy as jnp

D = 8192
FF = 28672
RANK = 16
SILOS = 64
STACKED = 1024


def touch_ends(values, stream_key, low, top_value):
    extent = values.shape
    index_at = [jax.random.randint(jax.random.fold_in(stream_key, axis), (), 0, extent[axis]) for axis in range(len(extent))]
    values = values.at[tuple(index_at)].set(low)
    longest = extent.index(max(extent))
    index_at[longest] = (index_at[longest] + 1) % extent[longest]
    return values.at[tuple(index_at)].set(top_value)


def level_of(stream_key, extent, pieces, least, largest):
    def one(position, parts):
        heights = jax.random.uniform(jax.random.fold_in(jax.random.fold_in(stream_key, 6), position), (parts,), jnp.float32, least / len(pieces), largest / len(pieces))
        return jnp.repeat(jnp.exp(heights), extent[position] // parts).reshape((-1,) + (1,) * (len(extent) - position - 1))

    factor_of = one(*pieces[0])
    for cut in pieces[1:]:
        factor_of = factor_of * one(*cut)
    return factor_of


def gaussian(rng, shape, spread, bound, split=(), kind=jnp.bfloat16):
    array = spread * jax.random.normal(rng, shape, jnp.float32)
    if split:
        array = array * level_of(rng, shape, split, -0.22, 0.18)
    return jnp.clip(array, -bound, bound).astype(kind)


def setup_inputs(seed: int = 0) -> dict:
    seeds = jax.random.split(jax.random.key(seed), 12)
    return {
        "sample_counts": touch_ends(jax.random.randint(seeds[0], (SILOS,), 100, 2001), jax.random.fold_in(seeds[0], 1), 100, 2000).astype(jnp.int32),
        "slot_silo": jax.random.permutation(seeds[1], SILOS).astype(jnp.int32),
        "gate_weight": gaussian(seeds[2], (FF, D), 0.5, 3.0, ((0, 8), (1, 4))),
        "up_weight": gaussian(seeds[3], (FF, D), 0.5, 3.0, ((0, 8), (1, 4))),
        "down_weight": gaussian(seeds[4], (D, FF), 0.5, 3.0, ((0, 8), (1, 4))),
        "gate_a": gaussian(seeds[5], (STACKED, D), 1.0, 6.0, ((0, 32),)),
        "up_a": gaussian(seeds[6], (STACKED, D), 1.0, 6.0, ((0, 32),)),
        "down_a": gaussian(seeds[7], (STACKED, FF), 1.0, 6.0, ((0, 32),)),
        "gate_b": gaussian(seeds[8], (STACKED, FF), 1.0, 6.0, ((0, 32),)),
        "up_b": gaussian(seeds[9], (STACKED, FF), 1.0, 6.0, ((0, 32),)),
        "down_b": gaussian(seeds[10], (STACKED, D), 1.0, 6.0, ((0, 32),)),
    }


def merge_one(weight, factor_a, factor_b, row_scale):
    scaled = (row_scale[:, None] * factor_a.astype(jnp.float32)).astype(jnp.bfloat16)
    update = jnp.dot(factor_b.T, scaled, preferred_element_type=jnp.float32)
    return (weight.astype(jnp.float32) + update).astype(jnp.bfloat16)


def reference(sample_counts, slot_silo, gate_weight, up_weight, down_weight, gate_a, up_a, down_a, gate_b, up_b, down_b):
    counts_f = sample_counts.astype(jnp.float32)
    shares = counts_f / jnp.sum(counts_f)
    slot_ids = (jnp.arange(SILOS * RANK, dtype=jnp.int32) // RANK).astype(jnp.int32)
    silo_ids = slot_silo[slot_ids]
    row_scale = shares[silo_ids]
    merged_gate = merge_one(gate_weight, gate_a, gate_b, row_scale)
    merged_up = merge_one(up_weight, up_a, up_b, row_scale)
    merged_down = merge_one(down_weight, down_a, down_b, row_scale)
    return (merged_gate, merged_up, merged_down)
```

```python
import functools

import jax
import jax.numpy as jnp
from jax import lax
from jax.experimental import pallas as pl
from jax.experimental.pallas import tpu as pltpu
from jax.sharding import PartitionSpec as P

RANK = 16
BLOCK = 256


def rows_scale(sample_counts, slot_silo, row_ids):
    slot_ids = row_ids // RANK
    silo_table = jnp.arange(slot_silo.shape[0], dtype=jnp.int32)
    silo_ids = jnp.sum(
        jnp.where(slot_ids[:, None] == silo_table[None, :], slot_silo[None, :], 0), axis=1
    )
    counts_f = sample_counts.astype(jnp.float32)
    shares = counts_f / jnp.sum(counts_f)
    return jnp.sum(
        jnp.where(silo_ids[:, None] == silo_table[None, :], shares[None, :], 0.0), axis=1
    )


def columns_of(array, index, parts):
    width = array.shape[1] // parts
    return lax.dynamic_slice_in_dim(array, index * width, width, axis=1)


def spread_rows(factor):
    n_row = lax.axis_size("row")
    mine = lax.axis_index("row")
    pieces = []
    for i in range(n_row):
        piece = columns_of(factor, mine ^ i, n_row)
        if i:
            piece = lax.ppermute(piece, "row", [(k, k ^ i) for k in range(n_row)])
        pieces.append(piece)
    return pieces


def spread_cols(factor):
    n_col = lax.axis_size("col")
    mine = lax.axis_index("col")
    pieces = []
    for s in range(n_col):
        piece = columns_of(factor, (mine + s) % n_col, n_col)
        if s:
            piece = lax.ppermute(piece, "col", [(j, (j + s) % n_col) for j in range(n_col)])
        pieces.append(piece)
    return pieces


def gather_rows(block):
    n_row = lax.axis_size("row")
    pieces = [None] * n_row
    pieces[0] = block
    for i in range(2, n_row, 2):
        pieces[i] = lax.ppermute(block, "row", [(k, k ^ i) for k in range(n_row)])
    for i in range(0, n_row, 2):
        pieces[i ^ 1] = lax.ppermute(pieces[i], "row", [(k, k ^ 1) for k in range(n_row)])
    return pieces


def merge_kernel(n_row, n_col, tile, *refs):
    b_ref, weight_ref = refs[:2]
    a_refs = refs[2 : 2 + n_row]
    out_ref, a_all, sems = refs[-3:]
    depth = a_refs[0].shape[0] // n_col

    @pl.when(pl.program_id(0) == 0)
    def _():
        mine = lax.axis_index("col")
        copies = []
        for s in range(n_col):
            owner = lax.rem(mine + (n_col - s), n_col)
            for i in range(n_row):
                start = pl.multiple_of(owner * (n_row * depth) + i * depth, depth)
                copies.append(
                    pltpu.make_async_copy(
                        a_refs[i].at[pl.ds(s * depth, depth)],
                        a_all.at[pl.ds(start, depth)],
                        sems.at[s * n_row + i],
                    )
                )
        for copy in copies:
            copy.start()
        for copy in copies:
            copy.wait()

    b = b_ref[...]
    for start in range(0, out_ref.shape[1], tile):
        at = slice(start, start + tile)
        update = lax.dot_general(
            b, a_all[:, at], (((0,), (0,)), ((), ())), preferred_element_type=jnp.float32
        )
        out_ref[:, at] = (weight_ref[:, at].astype(jnp.float32) + update).astype(out_ref.dtype)


def merge_rows(weight, b, a_pieces, first, done):
    n_row = lax.axis_size("row")
    n_col = lax.axis_size("col")
    rank, rows = b.shape
    width = weight.shape[1]
    skip = first // BLOCK
    tile = width
    while tile > 2048:
        tile //= 2
    operands = [b, weight, *a_pieces]
    in_specs = [
        pl.BlockSpec((rank, BLOCK), lambda g: (0, g)),
        pl.BlockSpec((BLOCK, width), lambda g: (g + skip, 0)),
    ] + [pl.BlockSpec(memory_space=pl.ANY)] * n_row
    aliases = {}
    if done is not None:
        aliases = {len(operands): 0}
        operands.append(done)
        in_specs.append(pl.BlockSpec(memory_space=pl.ANY))
    return pl.pallas_call(
        functools.partial(merge_kernel, n_row, n_col, tile),
        grid=(rows // BLOCK,),
        in_specs=in_specs,
        out_specs=pl.BlockSpec((BLOCK, width), lambda g: (g + skip, 0)),
        out_shape=jax.ShapeDtypeStruct(weight.shape, weight.dtype),
        scratch_shapes=[
            pltpu.VMEM((rank, width), jnp.bfloat16),
            pltpu.SemaphoreType.DMA((n_row * n_col,)),
        ],
        input_output_aliases=aliases,
        compiler_params=pltpu.CompilerParams(
            dimension_semantics=("arbitrary",), vmem_limit_bytes=60 * 1024 * 1024
        ),
        cost_estimate=pl.CostEstimate(
            flops=2 * rank * rows * width,
            bytes_accessed=2 * (rank * (rows + width) + 2 * rows * width),
            transcendentals=0,
        ),
    )(*operands)


def local(
    sample_counts,
    slot_silo,
    gate_weight,
    up_weight,
    down_weight,
    gate_a,
    up_a,
    down_a,
    gate_b,
    up_b,
    down_b,
):
    n_row = lax.axis_size("row")
    n_col = lax.axis_size("col")
    depth = gate_a.shape[0]

    down_spread = spread_rows(down_b)
    down_cols = spread_cols(down_a)
    gate_cols = spread_cols(gate_a)
    up_cols = spread_cols(up_a)
    down_mine, gate_b = lax.optimization_barrier((jnp.concatenate(down_spread), gate_b))
    gate_spread = spread_rows(gate_b)
    gate_mine, up_b = lax.optimization_barrier((jnp.concatenate(gate_spread), up_b))
    up_mine = jnp.concatenate(spread_rows(up_b))

    last = max(BLOCK, up_mine.shape[1] // 4 // BLOCK * BLOCK)
    early = up_mine.shape[1] - last
    down_whole = lax.all_gather(down_mine, "col", axis=0, tiled=True)
    gate_whole = lax.all_gather(gate_mine, "col", axis=0, tiled=True)
    up_whole = lax.all_gather(up_mine[:, :early], "col", axis=0, tiled=True)
    up_last = lax.all_gather(up_mine[:, early:], "col", axis=0, tiled=True)

    mine = lax.axis_index("col")
    owners = (mine + n_col - jnp.arange(n_col, dtype=jnp.int32)) % n_col
    shards = lax.axis_index("row") * n_col + owners
    row_ids = (shards[:, None] * depth + jnp.arange(depth, dtype=jnp.int32)[None, :]).reshape(-1)
    scale = rows_scale(sample_counts, slot_silo, row_ids)

    def gathered(cols):
        block = jnp.concatenate(cols)
        block = (scale[:, None] * block.astype(jnp.float32)).astype(jnp.bfloat16)
        return gather_rows(block)

    down_pieces = gathered(down_cols)
    gate_pieces = gathered(gate_cols)
    up_pieces = gathered(up_cols)

    merged_down = merge_rows(down_weight, down_whole, down_pieces, 0, None)
    merged_gate = merge_rows(gate_weight, gate_whole, gate_pieces, 0, None)
    merged_up = merge_rows(up_weight, up_whole, up_pieces, 0, None)
    merged_up = merge_rows(up_weight, up_last, up_pieces, early, merged_up)
    return merged_gate, merged_up, merged_down


def solution(mesh):
    return jax.shard_map(
        local,
        mesh=mesh,
        in_specs=(
            P(),
            P(),
            P("row", "col"),
            P("row", "col"),
            P("row", "col"),
            P(("row", "col"), None),
            P(("row", "col"), None),
            P(("row", "col"), None),
            P(("row", "col"), None),
            P(("row", "col"), None),
            P(("row", "col"), None),
        ),
        out_specs=(P("row", "col"), P("row", "col"), P("row", "col")),
        check_vma=False,
    )
```

```python
import functools

import jax
import jax.numpy as jnp
from jax import lax
from jax.experimental import pallas as pl
from jax.experimental.pallas import tpu as pltpu
from jax.sharding import PartitionSpec as P


RANK = 16
BLOCK = 256


def rows_scale(sample_counts, slot_silo, row_ids):
    slot_ids = row_ids // RANK
    silo_table = jnp.arange(slot_silo.shape[0], dtype=jnp.int32)
    silo_ids = jnp.sum(
        jnp.where(slot_ids[:, None] == silo_table[None, :], slot_silo[None, :], 0), axis=1
    )
    counts_f = sample_counts.astype(jnp.float32)
    shares = counts_f / jnp.sum(counts_f)
    return jnp.sum(
        jnp.where(silo_ids[:, None] == silo_table[None, :], shares[None, :], 0.0), axis=1
    )


def columns_of(array, index, parts):
    width = array.shape[1] // parts
    return lax.dynamic_slice_in_dim(array, index * width, width, axis=1)


def spread_rows(factors):
    n_row = lax.axis_size("row")
    mine = lax.axis_index("row")
    pieces = []
    for i in range(n_row):
        piece = jnp.concatenate([columns_of(f, mine ^ i, n_row) for f in factors], axis=1)
        if i:
            piece = lax.ppermute(piece, "row", [(k, k ^ i) for k in range(n_row)])
        pieces.append(piece)
    return jnp.concatenate(pieces)


def spread_cols(factors):
    n_col = lax.axis_size("col")
    mine = lax.axis_index("col")
    pieces = []
    for s in range(n_col):
        at = (mine + s) % n_col
        piece = jnp.concatenate([columns_of(f, at, n_col) for f in factors], axis=1)
        if s:
            piece = lax.ppermute(piece, "col", [(j, (j + s) % n_col) for j in range(n_col)])
        pieces.append(piece)
    return pieces


def gather_rows(block):
    n_row = lax.axis_size("row")
    pieces = [None] * n_row
    pieces[0] = block
    for i in range(2, n_row, 2):
        pieces[i] = lax.ppermute(block, "row", [(k, k ^ i) for k in range(n_row)])
    for i in range(0, n_row, 2):
        pieces[i ^ 1] = lax.ppermute(pieces[i], "row", [(k, k ^ 1) for k in range(n_row)])
    return pieces


def merge_kernel(n_row, n_col, tile, strides, column, *refs):
    b_ref, weight_ref = refs[:2]
    a_refs = refs[2 : 2 + n_row]
    out_ref, a_all, sems = refs[-3:]
    depth = a_refs[0].shape[0] // n_col
    row_stride, col_stride = strides

    @pl.when(pl.program_id(0) == 0)
    def _():
        mine = lax.axis_index("col")
        copies = []
        for s in range(n_col):
            owner = lax.rem(mine + (n_col - s), n_col)
            for i in range(n_row):
                start = pl.multiple_of(owner * col_stride + i * row_stride, depth)
                copies.append(
                    pltpu.make_async_copy(
                        a_refs[i].at[pl.ds(s * depth, depth), pl.ds(column, a_all.shape[1])],
                        a_all.at[pl.ds(start, depth)],
                        sems.at[s * n_row + i],
                    )
                )
        for copy in copies:
            copy.start()
        for copy in copies:
            copy.wait()

    b = b_ref[...]
    for start in range(0, out_ref.shape[1], tile):
        at = slice(start, start + tile)
        update = lax.dot_general(
            b, a_all[:, at], (((0,), (0,)), ((), ())), preferred_element_type=jnp.float32
        )
        out_ref[:, at] = (weight_ref[:, at].astype(jnp.float32) + update).astype(out_ref.dtype)


def merge_rows(weight, b, a_pieces, column, first=0, done=None, rows_outer=False):
    n_row = lax.axis_size("row")
    n_col = lax.axis_size("col")
    rank, rows = b.shape
    width = weight.shape[1]
    skip = first // BLOCK
    depth = rank // (n_row * n_col)
    strides = (n_col * depth, depth) if rows_outer else (depth, n_row * depth)
    tile = width
    while tile > 2048:
        tile //= 2
    operands = [b, weight, *a_pieces]
    in_specs = [
        pl.BlockSpec((rank, BLOCK), lambda g: (0, g)),
        pl.BlockSpec((BLOCK, width), lambda g: (g + skip, 0)),
    ] + [pl.BlockSpec(memory_space=pl.ANY)] * n_row
    aliases = {}
    if done is not None:
        aliases = {len(operands): 0}
        operands.append(done)
        in_specs.append(pl.BlockSpec(memory_space=pl.ANY))
    return pl.pallas_call(
        functools.partial(merge_kernel, n_row, n_col, tile, strides, column),
        grid=(rows // BLOCK,),
        in_specs=in_specs,
        out_specs=pl.BlockSpec((BLOCK, width), lambda g: (g + skip, 0)),
        out_shape=jax.ShapeDtypeStruct(weight.shape, weight.dtype),
        scratch_shapes=[
            pltpu.VMEM((rank, width), jnp.bfloat16),
            pltpu.SemaphoreType.DMA((n_row * n_col,)),
        ],
        input_output_aliases=aliases,
        compiler_params=pltpu.CompilerParams(
            dimension_semantics=("arbitrary",), vmem_limit_bytes=60 * 1024 * 1024
        ),
        cost_estimate=pl.CostEstimate(
            flops=2 * rank * rows * width,
            bytes_accessed=2 * (rank * (rows + width) + 2 * rows * width),
            transcendentals=0,
        ),
    )(*operands)


def local(
    sample_counts,
    slot_silo,
    gate_weight,
    up_weight,
    down_weight,
    gate_a,
    up_a,
    down_a,
    gate_b,
    up_b,
    down_b,
):
    n_col = lax.axis_size("col")
    depth = gate_a.shape[0]

    def whole_of(factor):
        return lax.all_gather(factor, "col", axis=0, tiled=True)

    down_raw = whole_of(down_b)
    cols = spread_cols((gate_a, up_a, down_a))
    mine_b = spread_rows((gate_b, up_b))
    down_whole = spread_rows((down_raw,))

    gate_rows, up_rows = gate_weight.shape[0], up_weight.shape[0]
    last = max(BLOCK, up_rows * 3 // 16 // BLOCK * BLOCK)
    cut = gate_rows + up_rows - last
    gate_whole = whole_of(mine_b[:, :gate_rows])
    up_whole = whole_of(mine_b[:, gate_rows:cut])
    up_last = whole_of(mine_b[:, cut:])

    mine = lax.axis_index("col")
    owners = (mine + n_col - jnp.arange(n_col, dtype=jnp.int32)) % n_col
    shards = lax.axis_index("row") * n_col + owners
    row_ids = (shards[:, None] * depth + jnp.arange(depth, dtype=jnp.int32)[None, :]).reshape(-1)
    scale = rows_scale(sample_counts, slot_silo, row_ids)

    gate_cols = gate_weight.shape[1]
    both_cols = gate_cols + up_weight.shape[1]

    def gathered(start, end):
        block = jnp.concatenate([piece[:, start:end] for piece in cols])
        block = (scale[:, None] * block.astype(jnp.float32)).astype(jnp.bfloat16)
        return gather_rows(block)

    down_pieces = gathered(both_cols, both_cols + down_weight.shape[1])
    mlp_pieces = gathered(0, both_cols)

    merged_down = merge_rows(down_weight, down_whole, down_pieces, 0, rows_outer=True)
    merged_gate = merge_rows(gate_weight, gate_whole, mlp_pieces, 0)
    merged_up = merge_rows(up_weight, up_whole, mlp_pieces, gate_cols)
    merged_up = merge_rows(up_weight, up_last, mlp_pieces, gate_cols, up_rows - last, merged_up)
    return merged_gate, merged_up, merged_down


def solution(mesh):
    return jax.shard_map(
        local,
        mesh=mesh,
        in_specs=(
            P(),
            P(),
            P("row", "col"),
            P("row", "col"),
            P("row", "col"),
            P(("row", "col"), None),
            P(("row", "col"), None),
            P(("row", "col"), None),
            P(("row", "col"), None),
            P(("row", "col"), None),
            P(("row", "col"), None),
        ),
        out_specs=(P("row", "col"), P("row", "col"), P("row", "col")),
        check_vma=False,
    )
```

```python
import functools

import jax
import jax.numpy as jnp
from jax import lax
from jax.experimental import pallas as pl
from jax.experimental.pallas import tpu as pltpu
from jax.sharding import PartitionSpec as P


RANK = 16
BLOCK = 512


def rows_scale(sample_counts, slot_silo, row_ids):
    slot_ids = row_ids // RANK
    silo_table = jnp.arange(slot_silo.shape[0], dtype=jnp.int32)
    silo_ids = jnp.sum(
        jnp.where(slot_ids[:, None] == silo_table[None, :], slot_silo[None, :], 0), axis=1
    )
    counts_f = sample_counts.astype(jnp.float32)
    shares = counts_f / jnp.sum(counts_f)
    return jnp.sum(
        jnp.where(silo_ids[:, None] == silo_table[None, :], shares[None, :], 0.0), axis=1
    )


def columns_of(array, index, parts):
    width = array.shape[1] // parts
    return lax.dynamic_slice_in_dim(array, index * width, width, axis=1)


def spread_rows(factors):
    n_row = lax.axis_size("row")
    mine = lax.axis_index("row")
    pieces = []
    for i in range(n_row):
        piece = jnp.concatenate([columns_of(f, mine ^ i, n_row) for f in factors], axis=1)
        if i:
            piece = lax.ppermute(piece, "row", [(k, k ^ i) for k in range(n_row)])
        pieces.append(piece)
    return pieces


def spread_cols(factors):
    n_col = lax.axis_size("col")
    mine = lax.axis_index("col")
    pieces = []
    for s in range(n_col):
        at = (mine + s) % n_col
        piece = jnp.concatenate([columns_of(f, at, n_col) for f in factors], axis=1)
        if s:
            piece = lax.ppermute(piece, "col", [(j, (j + s) % n_col) for j in range(n_col)])
        pieces.append(piece)
    return pieces


def gather_rows(block):
    n_row = lax.axis_size("row")
    pieces = [None] * n_row
    pieces[0] = block
    for i in range(2, n_row, 2):
        pieces[i] = lax.ppermute(block, "row", [(k, k ^ i) for k in range(n_row)])
    for i in range(0, n_row, 2):
        pieces[i ^ 1] = lax.ppermute(pieces[i], "row", [(k, k ^ 1) for k in range(n_row)])
    return pieces


def line_gather(block):
    n_col = lax.axis_size("col")
    up = down = block
    ups, downs = [None], [None]
    for s in range(1, n_col):
        up = lax.ppermute(up, "col", [(j, j + 1) for j in range(s - 1, n_col - 1)])
        down = lax.ppermute(down, "col", [(j, j - 1) for j in range(1, n_col + 1 - s)])
        ups.append(up)
        downs.append(down)
    return [(block,)] + [(ups[s], downs[n_col - s]) for s in range(1, n_col)]


def merge_kernel(n_row, n_col, block, tile, a_column, b_column, *refs):
    weight_ref = refs[0]
    a_refs = refs[1 : 1 + n_row]
    own_ref = refs[1 + n_row]
    pairs = refs[2 + n_row : 2 * n_col + n_row]
    out_ref, a_two, b_all, a_sems, b_sems = refs[-5:]
    depth = a_refs[0].shape[1]
    group = n_row * depth
    t, g = pl.program_id(0), pl.program_id(1)
    tiles, parts = pl.num_programs(0), b_sems.shape[0]

    def a_copies(t, slot):
        columns = pl.ds(pl.multiple_of(a_column + t * tile, 128), tile)
        return [
            pltpu.make_async_copy(
                a_refs[i].at[:, :, columns],
                a_two.at[slot, :, pl.ds(i * depth, depth)],
                a_sems.at[slot, i],
            )
            for i in range(n_row)
        ]

    def b_copy(ref, s, part):
        return pltpu.make_async_copy(
            ref.at[:, pl.ds(b_column + part * block, block)],
            b_all.at[part, pl.ds(s * group, group)],
            b_sems.at[part, s],
        )

    def b_start(part):
        mine = lax.axis_index("col")
        b_copy(own_ref, 0, part).start()
        for s in range(1, n_col):
            up_ref, down_ref = pairs[2 * (s - 1) : 2 * s]

            @pl.when(mine >= s)
            def _():
                b_copy(up_ref, s, part).start()

            @pl.when(mine < s)
            def _():
                b_copy(down_ref, s, part).start()

    @pl.when((t == 0) & (g == 0))
    def _():
        for copy in a_copies(0, 0):
            copy.start()
        for part in range(parts):
            b_start(part)

    @pl.when((g == 0) & (t + 1 < tiles))
    def _():
        for copy in a_copies(t + 1, lax.rem(t + 1, 2)):
            copy.start()

    @pl.when(t == 0)
    def _():
        for part in range(parts):

            @pl.when(g == part)
            def _():
                for s in range(n_col):
                    b_copy(own_ref, s, part).wait()

    slot = lax.rem(t, 2)

    @pl.when(g == 0)
    def _():
        for copy in a_copies(t, slot):
            copy.wait()

    update = lax.dot_general(
        b_all[g],
        a_two[slot].reshape(n_col * group, tile),
        (((0,), (0,)), ((), ())),
        preferred_element_type=jnp.float32,
    )
    out_ref[...] = (weight_ref[...].astype(jnp.float32) + update).astype(out_ref.dtype)


def merge_rows(weight, a_pieces, a_column, arrivals, b_column, first, rows, done=None):
    n_row = lax.axis_size("row")
    n_col = lax.axis_size("col")
    depth = a_pieces[0].shape[1]
    rank = n_row * n_col * depth
    width = weight.shape[1]
    block = next(b for b in range(896, 0, -128) if rows % b == 0 and first % b == 0)
    sizes = (512, 256, 128) if rows == block else (1024, 512, 256, 128)
    tile = next(size for size in sizes if width % size == 0)
    skip = first // block
    operands = [weight, *a_pieces]
    for arrival in arrivals:
        operands.extend(arrival)
    anywhere = pl.BlockSpec(memory_space=pl.ANY)
    spec = pl.BlockSpec((block, tile), lambda t, g: (g + skip, t))
    aliases = {}
    if done is not None:
        aliases = {len(operands): 0}
        operands.append(done)
    return pl.pallas_call(
        functools.partial(merge_kernel, n_row, n_col, block, tile, a_column, b_column),
        grid=(width // tile, rows // block),
        in_specs=[spec] + [anywhere] * (len(operands) - 1),
        out_specs=spec,
        out_shape=jax.ShapeDtypeStruct(weight.shape, weight.dtype),
        scratch_shapes=[
            pltpu.VMEM((2, n_col, n_row * depth, tile), jnp.bfloat16),
            pltpu.VMEM((rows // block, rank, block), jnp.bfloat16),
            pltpu.SemaphoreType.DMA((2, n_row)),
            pltpu.SemaphoreType.DMA((rows // block, n_col)),
        ],
        input_output_aliases=aliases,
        compiler_params=pltpu.CompilerParams(
            dimension_semantics=("arbitrary", "arbitrary"), vmem_limit_bytes=60 * 1024 * 1024
        ),
        cost_estimate=pl.CostEstimate(
            flops=2 * rank * rows * width,
            bytes_accessed=2 * (rank * (rows + width) + 2 * rows * width),
            transcendentals=0,
        ),
    )(*operands)


def shares_of(total, weights):
    unit = BLOCK
    while total % unit or total // unit < sum(weights):
        unit //= 2
    blocks = total // unit
    parts, left, rest = [], blocks, sum(weights)
    for weight in weights:
        part = left if weight == rest else max(1, left * weight // rest)
        part = min(part, left)
        parts.append(part * unit)
        left -= part
        rest -= weight
    return [part for part in parts if part]


def local(
    sample_counts,
    slot_silo,
    gate_weight,
    up_weight,
    down_weight,
    gate_a,
    up_a,
    down_a,
    gate_b,
    up_b,
    down_b,
):
    n_col = lax.axis_size("col")
    depth = gate_a.shape[0]

    cols = spread_cols((gate_a, up_a, down_a))
    gate_mine = jnp.concatenate(spread_rows((gate_b,)))
    rest_mine = jnp.concatenate(spread_rows((down_b, up_b)))

    mine = lax.axis_index("col")
    owners = (mine + n_col - jnp.arange(n_col, dtype=jnp.int32)) % n_col
    shards = lax.axis_index("row") * n_col + owners
    row_ids = (shards[:, None] * depth + jnp.arange(depth, dtype=jnp.int32)[None, :]).reshape(-1)
    scale = rows_scale(sample_counts, slot_silo, row_ids)

    gate_cols = gate_weight.shape[1]
    both_cols = gate_cols + up_weight.shape[1]

    def gathered(start, end):
        block = jnp.concatenate([piece[:, start:end] for piece in cols])
        block = (scale[:, None] * block.astype(jnp.float32)).astype(jnp.bfloat16)
        return gather_rows(block.reshape(n_col, depth, end - start))

    mlp_pieces = gathered(0, both_cols)
    down_pieces = gathered(both_cols, both_cols + down_weight.shape[1])

    down_rows = down_weight.shape[0]

    def merged(weight, a_pieces, a_column, source, start, weights):
        done, first = None, 0
        for rows in shares_of(weight.shape[0], weights):
            at = start + first
            arrivals = line_gather(source[:, at : at + rows])
            done = merge_rows(weight, a_pieces, a_column, arrivals, 0, first, rows, done)
            first += rows
        return done

    merged_gate = merged(gate_weight, mlp_pieces, 0, gate_mine, 0, (1, 1))
    merged_up = merged(up_weight, mlp_pieces, gate_cols, rest_mine, down_rows, (4, 3))

    arrivals = line_gather(rest_mine[:, :down_rows])
    merged_down = merge_rows(down_weight, down_pieces, 0, arrivals, 0, 0, down_rows)
    return merged_gate, merged_up, merged_down


def solution(mesh):
    return jax.shard_map(
        local,
        mesh=mesh,
        in_specs=(
            P(),
            P(),
            P("row", "col"),
            P("row", "col"),
            P("row", "col"),
            P(("row", "col"), None),
            P(("row", "col"), None),
            P(("row", "col"), None),
            P(("row", "col"), None),
            P(("row", "col"), None),
            P(("row", "col"), None),
        ),
        out_specs=(P("row", "col"), P("row", "col"), P("row", "col")),
        check_vma=False,
    )
```

```python
import functools

import jax
import jax.numpy as jnp
from jax import lax
from jax.experimental import pallas as pl
from jax.experimental.pallas import tpu as pltpu
from jax.sharding import PartitionSpec as P


RANK = 16
BLOCK = 512


def rows_scale(sample_counts, slot_silo, row_ids):
    slot_ids = row_ids // RANK
    silo_table = jnp.arange(slot_silo.shape[0], dtype=jnp.int32)
    silo_ids = jnp.sum(
        jnp.where(slot_ids[:, None] == silo_table[None, :], slot_silo[None, :], 0), axis=1
    )
    counts_f = sample_counts.astype(jnp.float32)
    shares = counts_f / jnp.sum(counts_f)
    return jnp.sum(
        jnp.where(silo_ids[:, None] == silo_table[None, :], shares[None, :], 0.0), axis=1
    )


def columns_of(array, index, parts):
    width = array.shape[1] // parts
    return lax.dynamic_slice_in_dim(array, index * width, width, axis=1)


def spread_rows(factors):
    n_row = lax.axis_size("row")
    mine = lax.axis_index("row")
    pieces = []
    for i in range(n_row):
        piece = jnp.concatenate([columns_of(f, mine ^ i, n_row) for f in factors], axis=1)
        if i:
            piece = lax.ppermute(piece, "row", [(k, k ^ i) for k in range(n_row)])
        pieces.append(piece)
    return pieces


def spread_cols(factors):
    n_col = lax.axis_size("col")
    mine = lax.axis_index("col")
    pieces = [None] * n_col
    for s in reversed(range(n_col)):
        piece = jnp.concatenate([columns_of(f, mine ^ s, n_col) for f in factors], axis=1)
        if s:
            piece = lax.ppermute(piece, "col", [(j, j ^ s) for j in range(n_col)])
        pieces[s] = piece
    return pieces


def gather_rows(block):
    n_row = lax.axis_size("row")
    pieces = [None] * n_row
    pieces[0] = block
    for i in range(2, n_row, 2):
        pieces[i] = lax.ppermute(block, "row", [(k, k ^ i) for k in range(n_row)])
    for i in range(0, n_row, 2):
        pieces[i ^ 1] = lax.ppermute(pieces[i], "row", [(k, k ^ 1) for k in range(n_row)])
    return pieces


def line_gather(block):
    n_col = lax.axis_size("col")
    up = down = block
    ups, downs = [None], [None]
    for s in range(1, n_col):
        up = lax.ppermute(up, "col", [(j, j + 1) for j in range(s - 1, n_col - 1)])
        down = lax.ppermute(down, "col", [(j, j - 1) for j in range(1, n_col + 1 - s)])
        ups.append(up)
        downs.append(down)
    return [(block,)] + [(ups[s], downs[n_col - s]) for s in range(1, n_col)]


def merge_kernel(n_row, n_col, block, tile, a_column, b_column, have, *refs):
    weight_ref = refs[0]
    a_refs = refs[1 : 1 + n_row]
    own_ref = refs[1 + n_row]
    came = iter(refs[2 + n_row :])
    came = [next(came) if there else None for there in have]
    out_ref, a_two, b_all, a_sems, b_sems = refs[-5:]
    depth = a_refs[0].shape[1]
    group = n_row * depth
    t, g = pl.program_id(0), pl.program_id(1)
    tiles, parts = pl.num_programs(0), b_sems.shape[0]

    def a_copies(t, slot):
        columns = pl.ds(pl.multiple_of(a_column + t * tile, 128), tile)
        return [
            pltpu.make_async_copy(
                a_refs[i].at[:, :, columns],
                a_two.at[slot, :, pl.ds(i * depth, depth)],
                a_sems.at[slot, i],
            )
            for i in range(n_row)
        ]

    def place(s):
        mine = lax.axis_index("col")
        slab = mine ^ lax.rem(mine + (n_col - s), n_col)
        return pl.ds(pl.multiple_of(slab * group, group), group)

    def b_copy(ref, s, part):
        return pltpu.make_async_copy(
            ref.at[:, pl.ds(b_column + part * block, block)],
            b_all.at[part, place(s)],
            b_sems.at[part, s],
        )

    def b_each(part, act):
        mine = lax.axis_index("col")
        act(own_ref, 0, part)
        for s in range(1, n_col):
            up_ref, down_ref = came[2 * (s - 1) : 2 * s]

            @pl.when(mine >= s)
            def _():
                act(up_ref, s, part)

            @pl.when(mine < s)
            def _():
                act(down_ref, s, part)

    def b_start(ref, s, part):
        if ref is None:
            b_all[part, place(s)] = jnp.zeros((group, block), b_all.dtype)
        else:
            b_copy(ref, s, part).start()

    def b_wait(ref, s, part):
        if ref is not None:
            b_copy(ref, s, part).wait()

    @pl.when((t == 0) & (g == 0))
    def _():
        for copy in a_copies(0, 0):
            copy.start()
        for part in range(parts):
            b_each(part, b_start)

    @pl.when((g == 0) & (t + 1 < tiles))
    def _():
        for copy in a_copies(t + 1, lax.rem(t + 1, 2)):
            copy.start()

    @pl.when(t == 0)
    def _():
        for part in range(parts):

            @pl.when(g == part)
            def _():
                b_each(part, b_wait)

    slot = lax.rem(t, 2)

    @pl.when(g == 0)
    def _():
        for copy in a_copies(t, slot):
            copy.wait()

    update = lax.dot_general(
        b_all[g],
        a_two[slot].reshape(n_col * group, tile),
        (((0,), (0,)), ((), ())),
        preferred_element_type=jnp.float32,
    )
    out_ref[...] = (weight_ref[...].astype(jnp.float32) + update).astype(out_ref.dtype)


def finish_kernel(n_row, n_col, block, tile, a_column, *refs):
    part_ref = refs[0]
    a_refs = refs[1 : 1 + n_row]
    up_ref, down_ref = refs[1 + n_row : 3 + n_row]
    out_ref, a_two, b_all, a_sems, b_sems = refs[-5:]
    depth = a_refs[0].shape[1]
    t, g = pl.program_id(0), pl.program_id(1)
    tiles, parts = pl.num_programs(0), b_sems.shape[0]
    mine = lax.axis_index("col")

    def a_copies(t, slot):
        columns = pl.ds(pl.multiple_of(a_column + t * tile, 128), tile)
        return [
            pltpu.make_async_copy(
                a_refs[i].at[n_col - 1, :, columns],
                a_two.at[slot, pl.ds(i * depth, depth)],
                a_sems.at[slot, i],
            )
            for i in range(n_row)
        ]

    def b_copy(ref, part):
        return pltpu.make_async_copy(
            ref.at[:, pl.ds(part * block, block)], b_all.at[part], b_sems.at[part]
        )

    @pl.when((t == 0) & (g == 0))
    def _():
        for copy in a_copies(0, 0):
            copy.start()

        @pl.when(mine == n_col - 1)
        def _():
            for part in range(parts):
                b_copy(up_ref, part).start()

        @pl.when(mine != n_col - 1)
        def _():
            for part in range(parts):
                b_copy(down_ref, part).start()

    @pl.when((g == 0) & (t + 1 < tiles))
    def _():
        for copy in a_copies(t + 1, lax.rem(t + 1, 2)):
            copy.start()

    @pl.when(t == 0)
    def _():
        for part in range(parts):

            @pl.when(g == part)
            def _():
                b_copy(up_ref, part).wait()

    slot = lax.rem(t, 2)

    @pl.when(g == 0)
    def _():
        for copy in a_copies(t, slot):
            copy.wait()

    update = lax.dot_general(
        b_all[g], a_two[slot], (((0,), (0,)), ((), ())), preferred_element_type=jnp.float32
    )
    out_ref[...] = (part_ref[...].astype(jnp.float32) + update).astype(out_ref.dtype)


def finish_rows(done, a_pieces, a_column, arrival, first, rows):
    n_row = lax.axis_size("row")
    n_col = lax.axis_size("col")
    depth = a_pieces[0].shape[1]
    width = done.shape[1]
    block = next(b for b in range(896, 0, -128) if rows % b == 0 and first % b == 0)
    tile = next(size for size in (1024, 512, 256, 128) if width % size == 0)
    skip = first // block
    anywhere = pl.BlockSpec(memory_space=pl.ANY)
    spec = pl.BlockSpec((block, tile), lambda t, g: (g + skip, t))
    return pl.pallas_call(
        functools.partial(finish_kernel, n_row, n_col, block, tile, a_column),
        grid=(width // tile, rows // block),
        in_specs=[spec] + [anywhere] * (n_row + 2),
        out_specs=spec,
        out_shape=jax.ShapeDtypeStruct(done.shape, done.dtype),
        scratch_shapes=[
            pltpu.VMEM((2, n_row * depth, tile), jnp.bfloat16),
            pltpu.VMEM((rows // block, n_row * depth, block), jnp.bfloat16),
            pltpu.SemaphoreType.DMA((2, n_row)),
            pltpu.SemaphoreType.DMA((rows // block,)),
        ],
        input_output_aliases={0: 0},
        compiler_params=pltpu.CompilerParams(
            dimension_semantics=("arbitrary", "arbitrary"), vmem_limit_bytes=60 * 1024 * 1024
        ),
        cost_estimate=pl.CostEstimate(
            flops=2 * n_row * depth * rows * width,
            bytes_accessed=4 * rows * width,
            transcendentals=0,
        ),
    )(done, *a_pieces, *arrival)


def merge_rows(weight, a_pieces, a_column, arrivals, b_column, first, rows, done=None):
    n_row = lax.axis_size("row")
    n_col = lax.axis_size("col")
    depth = a_pieces[0].shape[1]
    rank = n_row * n_col * depth
    width = weight.shape[1]
    block = next(b for b in range(896, 0, -128) if rows % b == 0 and first % b == 0)
    sizes = (512, 256, 128) if rows == block else (1024, 512, 256, 128)
    tile = next(size for size in sizes if width % size == 0)
    skip = first // block
    operands = [weight, *a_pieces, arrivals[0][0]]
    came = [array for arrival in arrivals[1:] for array in arrival]
    have = tuple(array is not None for array in came)
    operands.extend(array for array in came if array is not None)
    anywhere = pl.BlockSpec(memory_space=pl.ANY)
    spec = pl.BlockSpec((block, tile), lambda t, g: (g + skip, t))
    aliases = {}
    if done is not None:
        aliases = {len(operands): 0}
        operands.append(done)
    return pl.pallas_call(
        functools.partial(merge_kernel, n_row, n_col, block, tile, a_column, b_column, have),
        grid=(width // tile, rows // block),
        in_specs=[spec] + [anywhere] * (len(operands) - 1),
        out_specs=spec,
        out_shape=jax.ShapeDtypeStruct(weight.shape, weight.dtype),
        scratch_shapes=[
            pltpu.VMEM((2, n_col, n_row * depth, tile), jnp.bfloat16),
            pltpu.VMEM((rows // block, rank, block), jnp.bfloat16),
            pltpu.SemaphoreType.DMA((2, n_row)),
            pltpu.SemaphoreType.DMA((rows // block, n_col)),
        ],
        input_output_aliases=aliases,
        compiler_params=pltpu.CompilerParams(
            dimension_semantics=("arbitrary", "arbitrary"), vmem_limit_bytes=60 * 1024 * 1024
        ),
        cost_estimate=pl.CostEstimate(
            flops=2 * rank * rows * width,
            bytes_accessed=2 * (rank * (rows + width) + 2 * rows * width),
            transcendentals=0,
        ),
    )(*operands)


def shares_of(total, weights):
    unit = BLOCK
    while total % unit or total // unit < sum(weights):
        unit //= 2
    blocks = total // unit
    parts, left, rest = [], blocks, sum(weights)
    for weight in weights:
        part = left if weight == rest else max(1, left * weight // rest)
        part = min(part, left)
        parts.append(part * unit)
        left -= part
        rest -= weight
    return [part for part in parts if part]


def local(
    sample_counts,
    slot_silo,
    gate_weight,
    up_weight,
    down_weight,
    gate_a,
    up_a,
    down_a,
    gate_b,
    up_b,
    down_b,
):
    n_col = lax.axis_size("col")
    depth = gate_a.shape[0]

    cols = spread_cols((gate_a, up_a, down_a))
    gate_mine = jnp.concatenate(spread_rows((gate_b,)))
    rest_mine = jnp.concatenate(spread_rows((down_b, up_b)))

    mine = lax.axis_index("col")
    owners = mine ^ jnp.arange(n_col, dtype=jnp.int32)
    shards = lax.axis_index("row") * n_col + owners
    row_ids = (shards[:, None] * depth + jnp.arange(depth, dtype=jnp.int32)[None, :]).reshape(-1)
    scale = rows_scale(sample_counts, slot_silo, row_ids)

    gate_cols = gate_weight.shape[1]
    both_cols = gate_cols + up_weight.shape[1]

    def gathered(start, end):
        block = jnp.concatenate([piece[:, start:end] for piece in cols])
        block = (scale[:, None] * block.astype(jnp.float32)).astype(jnp.bfloat16)
        return gather_rows(block.reshape(n_col, depth, end - start))

    mlp_pieces = gathered(0, both_cols)
    down_pieces = gathered(both_cols, both_cols + down_weight.shape[1])

    down_rows = down_weight.shape[0]

    def merged(weight, a_pieces, a_column, source, start, weights, split=False):
        done, first = None, 0
        for rows in shares_of(weight.shape[0], weights):
            at = start + first
            arrivals = line_gather(source[:, at : at + rows])
            late = None
            if split and first + rows == weight.shape[0] and n_col > 2:
                late = arrivals[-1][0], arrivals[1][1]
                arrivals[-1] = None, arrivals[-1][1]
                arrivals[1] = arrivals[1][0], None
            done = merge_rows(weight, a_pieces, a_column, arrivals, 0, first, rows, done)
            if late:
                done = finish_rows(done, a_pieces, a_column, late, first, rows)
            first += rows
        return done

    merged_gate = merged(gate_weight, mlp_pieces, 0, gate_mine, 0, (1, 1))
    merged_up = merged(up_weight, mlp_pieces, gate_cols, rest_mine, down_rows, (4, 3), True)

    arrivals = line_gather(rest_mine[:, :down_rows])
    merged_down = merge_rows(down_weight, down_pieces, 0, arrivals, 0, 0, down_rows)
    return merged_gate, merged_up, merged_down


def solution(mesh):
    return jax.shard_map(
        local,
        mesh=mesh,
        in_specs=(
            P(),
            P(),
            P("row", "col"),
            P("row", "col"),
            P("row", "col"),
            P(("row", "col"), None),
            P(("row", "col"), None),
            P(("row", "col"), None),
            P(("row", "col"), None),
            P(("row", "col"), None),
            P(("row", "col"), None),
        ),
        out_specs=(P("row", "col"), P("row", "col"), P("row", "col")),
        check_vma=False,
    )
```

```python
import functools

import jax
import jax.numpy as jnp
from jax import lax
from jax.experimental import pallas as pl
from jax.experimental.pallas import tpu as pltpu
from jax.sharding import PartitionSpec as P


RANK = 16
BLOCK = 512


def rows_scale(sample_counts, slot_silo, row_ids):
    slot_ids = row_ids // RANK
    silo_table = jnp.arange(slot_silo.shape[0], dtype=jnp.int32)
    silo_ids = jnp.sum(
        jnp.where(slot_ids[:, None] == silo_table[None, :], slot_silo[None, :], 0), axis=1
    )
    counts_f = sample_counts.astype(jnp.float32)
    shares = counts_f / jnp.sum(counts_f)
    return jnp.sum(
        jnp.where(silo_ids[:, None] == silo_table[None, :], shares[None, :], 0.0), axis=1
    )


def columns_of(array, index, parts):
    width = array.shape[1] // parts
    return lax.dynamic_slice_in_dim(array, index * width, width, axis=1)


def spread_rows(factors):
    n_row = lax.axis_size("row")
    mine = lax.axis_index("row")
    pieces = []
    for i in range(n_row):
        piece = jnp.concatenate([columns_of(f, mine ^ i, n_row) for f in factors], axis=1)
        if i:
            piece = lax.ppermute(piece, "row", [(k, k ^ i) for k in range(n_row)])
        pieces.append(piece)
    return pieces


def spread_cols(factors):
    n_col = lax.axis_size("col")
    mine = lax.axis_index("col")
    pieces = [None] * n_col
    for s in reversed(range(n_col)):
        piece = jnp.concatenate([columns_of(f, mine ^ s, n_col) for f in factors], axis=1)
        if s:
            piece = lax.ppermute(piece, "col", [(j, j ^ s) for j in range(n_col)])
        pieces[s] = piece
    return pieces


def gather_rows(block):
    n_row = lax.axis_size("row")
    pieces = [None] * n_row
    pieces[0] = block
    for i in range(2, n_row, 2):
        pieces[i] = lax.ppermute(block, "row", [(k, k ^ i) for k in range(n_row)])
    for i in range(0, n_row, 2):
        pieces[i ^ 1] = lax.ppermute(pieces[i], "row", [(k, k ^ 1) for k in range(n_row)])
    return pieces


def line_gather(block):
    n_col = lax.axis_size("col")
    up = down = block
    ups, downs = [None], [None]
    for s in range(1, n_col):
        up = lax.ppermute(up, "col", [(j, j + 1) for j in range(s - 1, n_col - 1)])
        down = lax.ppermute(down, "col", [(j, j - 1) for j in range(1, n_col + 1 - s)])
        ups.append(up)
        downs.append(down)
    return [(block,)] + [(ups[s], downs[n_col - s]) for s in range(1, n_col)]


def merge_kernel(n_row, n_col, block, tile, a_column, b_column, have, *refs):
    weight_ref = refs[0]
    a_refs = refs[1 : 1 + n_row]
    own_ref = refs[1 + n_row]
    came = iter(refs[2 + n_row :])
    came = [next(came) if there else None for there in have]
    out_ref, a_two, b_all, a_sems, b_sems = refs[-5:]
    depth = a_refs[0].shape[1]
    group = n_row * depth
    t, g = pl.program_id(0), pl.program_id(1)
    tiles, parts = pl.num_programs(0), b_sems.shape[0]

    def a_copies(t, slot):
        columns = pl.ds(pl.multiple_of(a_column + t * tile, 128), tile)
        return [
            pltpu.make_async_copy(
                a_refs[i].at[:, :, columns],
                a_two.at[slot, :, pl.ds(i * depth, depth)],
                a_sems.at[slot, i],
            )
            for i in range(n_row)
        ]

    def place(s):
        mine = lax.axis_index("col")
        slab = mine ^ lax.rem(mine + (n_col - s), n_col)
        return pl.ds(pl.multiple_of(slab * group, group), group)

    def b_copy(ref, s, part):
        return pltpu.make_async_copy(
            ref.at[:, pl.ds(b_column + part * block, block)],
            b_all.at[part, place(s)],
            b_sems.at[part, s],
        )

    def b_each(part, act):
        mine = lax.axis_index("col")
        act(own_ref, 0, part)
        for s in range(1, n_col):
            up_ref, down_ref = came[2 * (s - 1) : 2 * s]

            @pl.when(mine >= s)
            def _():
                act(up_ref, s, part)

            @pl.when(mine < s)
            def _():
                act(down_ref, s, part)

    def b_start(ref, s, part):
        if ref is None:
            b_all[part, place(s)] = jnp.zeros((group, block), b_all.dtype)
        else:
            b_copy(ref, s, part).start()

    def b_wait(ref, s, part):
        if ref is not None:
            b_copy(ref, s, part).wait()

    @pl.when((t == 0) & (g == 0))
    def _():
        for copy in a_copies(0, 0):
            copy.start()
        for part in range(parts):
            b_each(part, b_start)

    @pl.when((g == 0) & (t + 1 < tiles))
    def _():
        for copy in a_copies(t + 1, lax.rem(t + 1, 2)):
            copy.start()

    @pl.when(t == 0)
    def _():
        for part in range(parts):

            @pl.when(g == part)
            def _():
                b_each(part, b_wait)

    slot = lax.rem(t, 2)

    @pl.when(g == 0)
    def _():
        for copy in a_copies(t, slot):
            copy.wait()

    update = lax.dot_general(
        b_all[g],
        a_two[slot].reshape(n_col * group, tile),
        (((0,), (0,)), ((), ())),
        preferred_element_type=jnp.float32,
    )
    out_ref[...] = (weight_ref[...].astype(jnp.float32) + update).astype(out_ref.dtype)


def finish_kernel(n_row, n_col, block, tile, a_column, *refs):
    part_ref = refs[0]
    a_refs = refs[1 : 1 + n_row]
    up_ref, down_ref = refs[1 + n_row : 3 + n_row]
    out_ref, a_two, b_all, a_sems, b_sems = refs[-5:]
    depth = a_refs[0].shape[1]
    t, g = pl.program_id(0), pl.program_id(1)
    tiles, parts = pl.num_programs(0), b_sems.shape[0]
    mine = lax.axis_index("col")

    def a_copies(t, slot):
        columns = pl.ds(pl.multiple_of(a_column + t * tile, 128), tile)
        return [
            pltpu.make_async_copy(
                a_refs[i].at[n_col - 1, :, columns],
                a_two.at[slot, pl.ds(i * depth, depth)],
                a_sems.at[slot, i],
            )
            for i in range(n_row)
        ]

    def b_copy(ref, part):
        return pltpu.make_async_copy(
            ref.at[:, pl.ds(part * block, block)], b_all.at[part], b_sems.at[part]
        )

    @pl.when((t == 0) & (g == 0))
    def _():
        for copy in a_copies(0, 0):
            copy.start()

        @pl.when(mine == n_col - 1)
        def _():
            for part in range(parts):
                b_copy(up_ref, part).start()

        @pl.when(mine != n_col - 1)
        def _():
            for part in range(parts):
                b_copy(down_ref, part).start()

    @pl.when((g == 0) & (t + 1 < tiles))
    def _():
        for copy in a_copies(t + 1, lax.rem(t + 1, 2)):
            copy.start()

    @pl.when(t == 0)
    def _():
        for part in range(parts):

            @pl.when(g == part)
            def _():
                b_copy(up_ref, part).wait()

    slot = lax.rem(t, 2)

    @pl.when(g == 0)
    def _():
        for copy in a_copies(t, slot):
            copy.wait()

    update = lax.dot_general(
        b_all[g], a_two[slot], (((0,), (0,)), ((), ())), preferred_element_type=jnp.float32
    )
    out_ref[...] = (part_ref[...].astype(jnp.float32) + update).astype(out_ref.dtype)


def finish_rows(done, a_pieces, a_column, arrival, first, rows):
    n_row = lax.axis_size("row")
    n_col = lax.axis_size("col")
    depth = a_pieces[0].shape[1]
    width = done.shape[1]
    block = next(b for b in (256, 128) if rows % b == 0 and first % b == 0)
    tile = next(size for size in (2048, 1024, 512, 256, 128) if width % size == 0)
    skip = first // block
    anywhere = pl.BlockSpec(memory_space=pl.ANY)
    spec = pl.BlockSpec((block, tile), lambda t, g: (g + skip, t))
    return pl.pallas_call(
        functools.partial(finish_kernel, n_row, n_col, block, tile, a_column),
        grid=(width // tile, rows // block),
        in_specs=[spec] + [anywhere] * (n_row + 2),
        out_specs=spec,
        out_shape=jax.ShapeDtypeStruct(done.shape, done.dtype),
        scratch_shapes=[
            pltpu.VMEM((2, n_row * depth, tile), jnp.bfloat16),
            pltpu.VMEM((rows // block, n_row * depth, block), jnp.bfloat16),
            pltpu.SemaphoreType.DMA((2, n_row)),
            pltpu.SemaphoreType.DMA((rows // block,)),
        ],
        input_output_aliases={0: 0},
        compiler_params=pltpu.CompilerParams(
            dimension_semantics=("arbitrary", "arbitrary"), vmem_limit_bytes=60 * 1024 * 1024
        ),
        cost_estimate=pl.CostEstimate(
            flops=2 * n_row * depth * rows * width,
            bytes_accessed=4 * rows * width,
            transcendentals=0,
        ),
    )(done, *a_pieces, *arrival)


def merge_rows(weight, a_pieces, a_column, arrivals, b_column, first, rows, done=None):
    n_row = lax.axis_size("row")
    n_col = lax.axis_size("col")
    depth = a_pieces[0].shape[1]
    rank = n_row * n_col * depth
    width = weight.shape[1]
    block = next(b for b in range(896, 0, -128) if rows % b == 0 and first % b == 0)
    sizes = (512, 256, 128) if rows == block else (1024, 512, 256, 128)
    tile = next(size for size in sizes if width % size == 0)
    skip = first // block
    operands = [weight, *a_pieces, arrivals[0][0]]
    came = [array for arrival in arrivals[1:] for array in arrival]
    have = tuple(array is not None for array in came)
    operands.extend(array for array in came if array is not None)
    anywhere = pl.BlockSpec(memory_space=pl.ANY)
    spec = pl.BlockSpec((block, tile), lambda t, g: (g + skip, t))
    aliases = {}
    if done is not None:
        aliases = {len(operands): 0}
        operands.append(done)
    return pl.pallas_call(
        functools.partial(merge_kernel, n_row, n_col, block, tile, a_column, b_column, have),
        grid=(width // tile, rows // block),
        in_specs=[spec] + [anywhere] * (len(operands) - 1),
        out_specs=spec,
        out_shape=jax.ShapeDtypeStruct(weight.shape, weight.dtype),
        scratch_shapes=[
            pltpu.VMEM((2, n_col, n_row * depth, tile), jnp.bfloat16),
            pltpu.VMEM((rows // block, rank, block), jnp.bfloat16),
            pltpu.SemaphoreType.DMA((2, n_row)),
            pltpu.SemaphoreType.DMA((rows // block, n_col)),
        ],
        input_output_aliases=aliases,
        compiler_params=pltpu.CompilerParams(
            dimension_semantics=("arbitrary", "arbitrary"), vmem_limit_bytes=60 * 1024 * 1024
        ),
        cost_estimate=pl.CostEstimate(
            flops=2 * rank * rows * width,
            bytes_accessed=2 * (rank * (rows + width) + 2 * rows * width),
            transcendentals=0,
        ),
    )(*operands)


def shares_of(total, weights):
    unit = BLOCK
    while total % unit or total // unit < sum(weights):
        unit //= 2
    blocks = total // unit
    parts, left, rest = [], blocks, sum(weights)
    for weight in weights:
        part = left if weight == rest else max(1, left * weight // rest)
        part = min(part, left)
        parts.append(part * unit)
        left -= part
        rest -= weight
    return [part for part in parts if part]


def local(
    sample_counts,
    slot_silo,
    gate_weight,
    up_weight,
    down_weight,
    gate_a,
    up_a,
    down_a,
    gate_b,
    up_b,
    down_b,
):
    n_col = lax.axis_size("col")
    depth = gate_a.shape[0]

    cols = spread_cols((gate_a, up_a, down_a))
    gate_mine = jnp.concatenate(spread_rows((gate_b,)))
    rest_mine = jnp.concatenate(spread_rows((down_b, up_b)))

    mine = lax.axis_index("col")
    owners = mine ^ jnp.arange(n_col, dtype=jnp.int32)
    shards = lax.axis_index("row") * n_col + owners
    row_ids = (shards[:, None] * depth + jnp.arange(depth, dtype=jnp.int32)[None, :]).reshape(-1)
    scale = rows_scale(sample_counts, slot_silo, row_ids)

    gate_cols = gate_weight.shape[1]
    both_cols = gate_cols + up_weight.shape[1]

    def gathered(start, end):
        block = jnp.concatenate([piece[:, start:end] for piece in cols])
        block = (scale[:, None] * block.astype(jnp.float32)).astype(jnp.bfloat16)
        return gather_rows(block.reshape(n_col, depth, end - start))

    mlp_pieces = gathered(0, both_cols)
    down_pieces = gathered(both_cols, both_cols + down_weight.shape[1])

    down_rows = down_weight.shape[0]

    def merged(weight, a_pieces, a_column, source, start, weights, split=False):
        done, first = None, 0
        for rows in shares_of(weight.shape[0], weights):
            at = start + first
            arrivals = line_gather(source[:, at : at + rows])
            late = None
            if split and first + rows == weight.shape[0] and n_col > 2:
                late = arrivals[-1][0], arrivals[1][1]
                arrivals[-1] = None, arrivals[-1][1]
                arrivals[1] = arrivals[1][0], None
            done = merge_rows(weight, a_pieces, a_column, arrivals, 0, first, rows, done)
            if late:
                done = finish_rows(done, a_pieces, a_column, late, first, rows)
            first += rows
        return done

    merged_gate = merged(gate_weight, mlp_pieces, 0, gate_mine, 0, (1, 1))
    merged_up = merged(up_weight, mlp_pieces, gate_cols, rest_mine, down_rows, (3, 4), True)

    arrivals = line_gather(rest_mine[:, :down_rows])
    merged_down = merge_rows(down_weight, down_pieces, 0, arrivals, 0, 0, down_rows)
    return merged_gate, merged_up, merged_down


def solution(mesh):
    return jax.shard_map(
        local,
        mesh=mesh,
        in_specs=(
            P(),
            P(),
            P("row", "col"),
            P("row", "col"),
            P("row", "col"),
            P(("row", "col"), None),
            P(("row", "col"), None),
            P(("row", "col"), None),
            P(("row", "col"), None),
            P(("row", "col"), None),
            P(("row", "col"), None),
        ),
        out_specs=(P("row", "col"), P("row", "col"), P("row", "col")),
        check_vma=False,
    )
```
